32 devices in a mesh: groups: 2 (over y), wide: 8 (over z, x), narrow: 2 (over core).
Axes of the slice: x: 2, y: 2, z: 4, core: 2. Of those that a mesh axis runs over, the one named last changes fastest.
Arguments:
- states: bfloat16 [2048, 32, 256], P(None, ('groups', 'wide', 'narrow')), parts along dimension 1, may hold values from -6 to 6
- var_weights: bfloat16 [4, 256, 256], replicated, may hold values from -0.375 to 0.375
- samp_weights: bfloat16 [4, 256, 256], replicated, may hold values from -0.375 to 0.375
- norm_gains: float32 [3, 256], replicated, may hold values from 0.25 to 1.75
- edge_weights: bfloat16 [2, 256, 256], replicated, may hold values from -0.375 to 0.375
- none_weight: bfloat16 [256], replicated, may hold values from -0.375 to 0.375
Outputs:
- edge_prob: float32 [6, 2048, 2048], P('groups', 'wide', 'narrow'), parts along dimension 0
The draws below stay inside these ranges and needn't reach their ends.
There are 2 independent parts, one for each index of `groups`. The reference program is written for one: setup_inputs(seed, part) draws one part's arguments, and reference() takes and returns one part's arrays. A program takes and returns all parts, laid end to end along the dimension named above; an argument that names none is the same for every part. Nothing has to cross between parts.
All inputs are finite; a program needn't handle non-finite values.
Results may differ from the reference program's by a relative error of at most 0.015.
The reference program's roundings to bfloat16 on the way count: a program that leaves them out, or rounds other values in their place, can miss the bound.
Values may be sent and summed in bfloat16 or wider, within the bound.
A program may use at most 64 MiB of HBM per device.

```python
import jax
import jax.numpy as jnp
from jax import lax

V = 2048
D = 256
HEADS = 8
S = 16


def steps_of(rng, extent, cuts, low, top_value):
    factor_of, own = 1.0, jax.random.fold_in(rng, 6)
    for dim, blocks in cuts:
        draws = jnp.exp(jax.random.uniform(jax.random.fold_in(own, dim), (blocks,), jnp.float32, low / len(cuts), top_value / len(cuts)))
        factor_of = factor_of * jnp.repeat(draws, extent[dim] // blocks).reshape([-1 if axis == dim else 1 for axis in range(len(extent))])
    return factor_of


def normal_values(key, extent, deviation, most, pieces=(), kind=jnp.bfloat16):
    drawn = jax.random.normal(key, extent, jnp.float32) * deviation
    if len(pieces) > 0:
        drawn = steps_of(key, extent, pieces, -0.22, 0.18) * drawn
    return jnp.clip(drawn, min=-most, max=most).astype(kind)


def setup_inputs(seed: int = 0, part: int = 0) -> dict:
    key_list = jax.random.split(jax.random.key(seed), 7)
    own_keys = jax.random.split(jax.random.fold_in(key_list[6], part), 7)
    states = normal_values(own_keys[0], (V, S, D), 1.0, 6.0, ((1, 16),))
    var_weights = normal_values(key_list[1], (4, D, D), D ** -0.5, 0.375)
    samp_weights = normal_values(key_list[2], (4, D, D), D ** -0.5, 0.375)
    norm_gains = jnp.clip(1.0 + 0.15 * jax.random.normal(key_list[3], (3, D), jnp.float32), 0.25, 1.75)
    edge_weights = normal_values(key_list[4], (2, D, D), D ** -0.5, 0.375)
    none_weight = normal_values(key_list[5], (D,), D ** -0.5, 0.375)
    return dict(states=states, var_weights=var_weights, samp_weights=samp_weights, norm_gains=norm_gains, edge_weights=edge_weights, none_weight=none_weight)


def layer_norm(values, gain):
    mean = lax.optimization_barrier(jnp.mean(values, axis=-1, keepdims=True))
    centered = values - mean
    var = lax.optimization_barrier(jnp.mean(centered * centered, axis=-1, keepdims=True))
    return centered * lax.rsqrt(var + 1e-05) * gain

def project(normed, weight):
    return jnp.dot(normed, weight, preferred_element_type=jnp.float32).astype(jnp.bfloat16)

def attend(seq, gain, weights):
    length = seq.shape[0]
    normed = layer_norm(seq.astype(jnp.float32), gain).astype(jnp.bfloat16)
    queries = project(normed, weights[0]).reshape(length, HEADS, -1).astype(jnp.float32)
    keys_all = project(normed, weights[1]).reshape(length, HEADS, -1).astype(jnp.float32)
    values_all = project(normed, weights[2]).reshape(length, HEADS, -1).astype(jnp.float32)
    scale = 1.0 / queries.shape[2] ** 0.5
    scores = jnp.einsum('qhd,khd->hqk', queries, keys_all) * scale
    expd = jnp.exp(scores)
    probs = (expd / lax.optimization_barrier(jnp.sum(expd, axis=2, keepdims=True))).astype(jnp.bfloat16)
    mixed = jnp.einsum('hqk,khd->qhd', probs.astype(jnp.float32), values_all)
    mixed = mixed.reshape(length, -1).astype(jnp.bfloat16)
    update = jnp.dot(mixed, weights[3], preferred_element_type=jnp.float32)
    return (seq.astype(jnp.float32) + update).astype(jnp.bfloat16)

def reference(states, var_weights, samp_weights, norm_gains, edge_weights, none_weight):
    by_sample = jnp.transpose(states, (1, 0, 2))
    mixed_var = lax.map(lambda seq: attend(seq, norm_gains[0], var_weights), by_sample)
    by_variable = jnp.transpose(mixed_var, (1, 0, 2))
    mixed_samp = lax.map(lambda seq: attend(seq, norm_gains[1], samp_weights), by_variable)
    pooled = lax.optimization_barrier(jnp.max(mixed_samp, axis=1))
    normed = layer_norm(pooled.astype(jnp.float32), norm_gains[2]).astype(jnp.bfloat16)
    source = project(normed, edge_weights[0])
    target = project(normed, edge_weights[1])
    none_term = jnp.dot(normed, none_weight, preferred_element_type=jnp.float32).astype(jnp.bfloat16)
    escale = 1.0 / source.shape[1] ** 0.5
    forward = jnp.dot(source, target.T, preferred_element_type=jnp.float32) * escale
    backward = jnp.dot(target, source.T, preferred_element_type=jnp.float32) * escale
    absent = none_term.astype(jnp.float32)[:, None] + none_term.astype(jnp.float32)[None, :]
    expd = jnp.exp(jnp.stack([forward, backward, absent]))
    return expd / lax.optimization_barrier(jnp.sum(expd, axis=0, keepdims=True))
```

```python
import functools
import math

import jax
import jax.numpy as jnp
from jax import lax
from jax.experimental import pallas as pl
from jax.experimental.pallas import tpu as pltpu
from jax.sharding import PartitionSpec as P

HEADS = 8
BLOCK = 128
KEYS = 256
F32, BF16 = jnp.float32, jnp.bfloat16
MESH = pl.DeviceIdType.MESH


def layer_norm(values, gain):
    mean = jnp.mean(values, axis=-1, keepdims=True)
    centered = values - mean
    var = jnp.mean(centered * centered, axis=-1, keepdims=True)
    return (centered * lax.rsqrt(var + 1e-05) * gain).astype(BF16)


def project(normed, weight):
    return jnp.dot(normed, weight, preferred_element_type=F32).astype(BF16)


def across(a, b):
    return lax.dot_general(a, b, (((1,), (1,)), ((), ())), preferred_element_type=F32)


def stack_heads(q, stacked):
    head = lax.broadcasted_iota(jnp.int32, q.shape, 1) // (q.shape[1] // HEADS)
    for h in range(HEADS):
        stacked[h * BLOCK : (h + 1) * BLOCK, :] = jnp.where(head == h, q, jnp.zeros_like(q))


def attend_block(stacked, keys_of, values_of, length, same):
    width = stacked.shape[1]
    step = min(KEYS, length)
    count = length // step
    factor = math.log2(math.e) / math.sqrt(width // HEADS)
    q = stacked[...]
    ahead = across(q, keys_of(0, step))
    acc = total = None
    for j in range(count):
        scores = ahead
        if j + 1 < count:
            ahead = across(q, keys_of((j + 1) * step, step))
        expd = jnp.exp2(scores * factor)
        if same is not None:
            expd = jnp.where(same, expd, 0.0)
        part = sum(expd[:, i : i + 128] for i in range(0, step, 128))
        total = part if total is None else total + part
        term = jnp.dot(expd.astype(BF16), values_of(j * step, step), preferred_element_type=F32)
        acc = term if acc is None else acc + term
    inverse = 4.0 / jnp.sum(total, axis=1, keepdims=True)
    acc = acc * inverse * 64.0
    head = lax.broadcasted_iota(jnp.int32, (BLOCK, width), 1) // (width // HEADS)
    out = acc[:BLOCK]
    for h in range(1, HEADS):
        out = jnp.where(head == h, acc[h * BLOCK : (h + 1) * BLOCK], out)
    return out.astype(BF16)


def mix_kernel(
    wide, narrow, x_ref, vw_ref, sw_ref, gain_ref, cols_ref, rows_ref,
    q_s, k_s, v_s, x_s, stacked, outbox, inbox, pooled, mine,
    send_a, recv_a, send_c, recv_c, send_r, recv_r,
):
    total_vars, width = x_ref.shape
    devices = wide * narrow
    own = total_vars // devices
    per_block = BLOCK // own
    blocks = total_vars // BLOCK
    my_wide, my_narrow = lax.axis_index("wide"), lax.axis_index("narrow")
    me = my_wide * narrow + my_narrow

    def device(d):
        return {"wide": d // narrow, "narrow": lax.rem(d, narrow)}

    barrier = pltpu.get_barrier_semaphore()

    def greet(d, carry):
        @pl.when(d != me)
        def _():
            pl.semaphore_signal(barrier, inc=1, device_id=device(d), device_id_type=MESH)

        return carry

    lax.fori_loop(0, devices, greet, 0)

    def keep(rows, normed, w_ref):
        q_s[rows, :] = project(normed, w_ref[0])
        k_s[rows, :] = project(normed, w_ref[1])
        v = project(normed, w_ref[2])
        v_s[rows, :] = (v.astype(F32) * 2.0**-8).astype(BF16)

    def prepare(i, carry):
        rows = pl.ds(pl.multiple_of(i * 256, 256), 256)
        keep(rows, layer_norm(x_ref[rows, :].astype(F32), gain_ref[0:1, :]), vw_ref)
        return carry

    lax.fori_loop(0, total_vars // 256, prepare, 0)

    my_block = me // per_block

    def post(block):
        def one(j, carry):
            d = block * per_block + j

            @pl.when(d != me)
            def _():
                pltpu.make_async_remote_copy(
                    src_ref=outbox.at[d], dst_ref=inbox.at[me],
                    send_sem=send_a.at[d], recv_sem=recv_a.at[me],
                    device_id=device(d), device_id_type=MESH,
                ).start()

            return carry

        lax.fori_loop(0, per_block, one, 0)

    def variable_block(t):
        block = lax.rem(my_block + 1 + t, blocks)
        rows = pl.ds(pl.multiple_of(block * BLOCK, BLOCK), BLOCK)
        stack_heads(q_s[rows, :], stacked.at[0])
        out = attend_block(
            stacked.at[0], lambda a, n: k_s[a : a + n, :], lambda a, n: v_s[a : a + n, :],
            total_vars, None,
        )
        update = jnp.dot(out, vw_ref[3], preferred_element_type=F32)
        mixed = x_ref[rows, :].astype(F32) + update
        outbox[pl.ds(block * per_block, per_block)] = mixed.reshape(per_block, own, width).astype(BF16)
        return block

    variable_block(0)
    pl.semaphore_wait(barrier, devices - 1)

    def variable_step(t, carry):
        post(lax.rem(my_block + t, blocks))
        variable_block(t)
        return carry

    lax.fori_loop(1, blocks, variable_step, 0)
    if per_block > 1:
        post(my_block)
    inbox[me] = outbox[me]

    def collect(d, carry):
        @pl.when(d != me)
        def _():
            pltpu.make_async_remote_copy(
                src_ref=outbox.at[d], dst_ref=inbox.at[d],
                send_sem=send_a.at[d], recv_sem=recv_a.at[d],
                device_id=device(d), device_id_type=MESH,
            ).wait()

        return carry

    lax.fori_loop(0, devices, collect, 0)

    tile = 8 * devices
    lump = 16 if own % 16 == 0 else 8

    def prepare_samples(i, carry):
        if lump == own:
            values = inbox[...].astype(F32)
        else:
            values = inbox[:, pl.ds(pl.multiple_of(i * lump, lump), lump), :].astype(F32)
        for half in range(lump // 8):
            start = (i * (lump // 8) + half) * tile
            rows = pl.ds(pl.multiple_of(start, tile), tile)
            tokens = values[:, half * 8 : half * 8 + 8, :].reshape(tile, width)
            x_s[rows, :] = tokens.astype(BF16)
            keep(rows, layer_norm(tokens, gain_ref[1:2, :]), sw_ref)
        return carry

    lax.fori_loop(0, own // lump, prepare_samples, 0)
    pooled[...] = jnp.full(pooled.shape, -jnp.inf, F32)
    step = min(KEYS, tile)
    row_var = lax.broadcasted_iota(jnp.int32, (HEADS * BLOCK, step), 0) % 8
    col_var = lax.broadcasted_iota(jnp.int32, (HEADS * BLOCK, step), 1) % 8
    same = row_var == col_var

    def sample_chunk(c, slot):
        rows = pl.ds(pl.multiple_of(c * BLOCK, BLOCK), BLOCK)
        base = c // (tile // BLOCK)
        stack_heads(q_s[rows, :], stacked.at[slot])

        def part(ref):
            return lambda a, n: ref[pl.ds(pl.multiple_of(base * tile + a, BLOCK), n), :]

        out = attend_block(stacked.at[slot], part(k_s), part(v_s), tile, same)
        update = jnp.dot(out, sw_ref[3], preferred_element_type=F32)
        mixed = (x_s[rows, :].astype(F32) + update).astype(BF16).astype(F32)
        best = jnp.max(mixed.reshape(BLOCK // 8, 8, width), axis=0)
        where = pl.ds(pl.multiple_of(base * 8, 8), 8)
        pooled[where, :] = jnp.maximum(pooled[where, :], best)

    piece = min(32, own)
    pieces = own // piece
    per_piece = piece * devices // BLOCK
    unroll = min(stacked.shape[0], per_piece)
    half = devices // narrow
    target = me // half
    slot = lax.rem(me, half)

    def to_cols(w, rows):
        return pltpu.make_async_remote_copy(
            src_ref=mine.at[rows], dst_ref=cols_ref.at[slot, rows],
            send_sem=send_c.at[w], recv_sem=recv_c.at[slot],
            device_id={"wide": w, "narrow": target}, device_id_type=MESH,
        )

    def to_rows(n, rows):
        return pltpu.make_async_remote_copy(
            src_ref=mine.at[rows], dst_ref=rows_ref.at[my_narrow, rows],
            send_sem=send_r.at[n], recv_sem=recv_r.at[my_narrow],
            device_id={"wide": my_wide, "narrow": n}, device_id_type=MESH,
        )

    def each_target(do, rows):
        def one(w, carry):
            @pl.when(w * narrow + target != me)
            def _():
                do(to_cols(w, rows))

            return carry

        lax.fori_loop(0, wide, one, 0)

        def other(n, carry):
            @pl.when(n != my_narrow)
            def _():
                do(to_rows(n, rows))

            return carry

        lax.fori_loop(0, narrow, other, 0)

    def piece_rows(g):
        return pl.ds(pl.multiple_of(g * piece, piece), piece)

    def sample_piece(g, carry):
        if pieces > 1:
            @pl.when(g > 0)
            def _():
                each_target(lambda copy: copy.start(), piece_rows(g - 1))

        def group(i, inner):
            for u in range(unroll):
                sample_chunk(g * per_piece + i * unroll + u, u)
            return inner

        if per_piece == unroll:
            group(0, 0)
        else:
            lax.fori_loop(0, per_piece // unroll, group, 0)
        rows = piece_rows(g)
        mine[rows, :] = layer_norm(pooled[rows, :], gain_ref[2:3, :])
        return carry

    lax.fori_loop(0, pieces, sample_piece, 0)
    each_target(lambda copy: copy.start(), piece_rows(pieces - 1))
    rows_ref[my_narrow] = mine[...]

    @pl.when(target == my_narrow)
    def _():
        cols_ref[slot] = mine[...]

    whole = pl.ds(0, own)
    each_target(lambda copy: copy.wait_send(), whole)

    def arrived(i, carry):
        @pl.when(my_narrow * half + i != me)
        def _():
            pltpu.make_async_remote_copy(
                src_ref=mine, dst_ref=cols_ref.at[i], send_sem=send_c.at[0],
                recv_sem=recv_c.at[i], device_id=device(me), device_id_type=MESH,
            ).wait_recv()

        return carry

    lax.fori_loop(0, half, arrived, 0)

    def beside(n, carry):
        @pl.when(n != my_narrow)
        def _():
            pltpu.make_async_remote_copy(
                src_ref=mine, dst_ref=rows_ref.at[n], send_sem=send_r.at[0],
                recv_sem=recv_r.at[n], device_id=device(me), device_id_type=MESH,
            ).wait_recv()

        return carry

    lax.fori_loop(0, narrow, beside, 0)


def edge_kernel(rows_ref, cols_ref, w_ref, none_ref, out_ref, src_s, dst_s, none_s):
    scale = 1.0 / rows_ref.shape[1] ** 0.5

    @pl.when(pl.program_id(0) == 0)
    def _():
        rows = rows_ref[...]
        src_s[...] = project(rows, w_ref[0])
        dst_s[...] = project(rows, w_ref[1])
        none_s[...] = across(rows, none_ref[...]).astype(BF16).astype(F32)

    cols = cols_ref[...]
    forward = jnp.exp(across(src_s[...], project(cols, w_ref[1])) * scale)
    backward = jnp.exp(across(dst_s[...], project(cols, w_ref[0])) * scale)
    none_cols = across(none_ref[...], cols).astype(BF16).astype(F32)
    absent = jnp.exp(none_s[:, 0:1] + none_cols[0:1, :])
    total = forward + backward + absent
    out_ref[0] = forward / total
    out_ref[1] = backward / total
    out_ref[2] = absent / total


def on_device(states, var_weights, samp_weights, norm_gains, edge_weights, none_weight):
    total_vars, samp_local, width = states.shape
    wide, narrow = lax.axis_size("wide"), lax.axis_size("narrow")
    devices = wide * narrow
    own = total_vars // devices
    assert samp_local == 1 and BLOCK % own == 0 and own % 8 == 0
    half = devices // narrow
    vmem = pl.BlockSpec(memory_space=pltpu.VMEM)
    dma = pltpu.SemaphoreType.DMA
    cols, rows = pl.pallas_call(
        functools.partial(mix_kernel, wide, narrow),
        out_shape=(
            jax.ShapeDtypeStruct((half, own, width), BF16),
            jax.ShapeDtypeStruct((narrow, own, width), BF16),
        ),
        in_specs=[vmem] * 4,
        out_specs=(vmem, vmem),
        scratch_shapes=[pltpu.VMEM((total_vars, width), BF16)] * 4
        + [
            pltpu.VMEM((4, HEADS * BLOCK, width), BF16),
            pltpu.VMEM((devices, own, width), BF16),
            pltpu.VMEM((devices, own, width), BF16),
            pltpu.VMEM((own, width), F32),
            pltpu.VMEM((own, width), BF16),
            dma((devices,)), dma((devices,)), dma((wide,)), dma((half,)),
            dma((narrow,)), dma((narrow,)),
        ],
        compiler_params=pltpu.CompilerParams(
            collective_id=0, has_side_effects=True, vmem_limit_bytes=60 * 2**20
        ),
        name="mix",
    )(states.reshape(total_vars, width), var_weights, samp_weights, norm_gains)
    cols = cols.reshape(half * own, width)
    rows = rows.reshape(narrow * own, width)
    row_count, col_count = narrow * own, half * own
    tile = min(256, col_count)
    none_rows = jnp.broadcast_to(none_weight[None, :], (16, width))
    return pl.pallas_call(
        edge_kernel,
        grid=(col_count // tile,),
        out_shape=jax.ShapeDtypeStruct((3, row_count, col_count), F32),
        in_specs=[
            pl.BlockSpec((row_count, width), lambda i: (0, 0)),
            pl.BlockSpec((tile, width), lambda i: (i, 0)),
            pl.BlockSpec((2, width, width), lambda i: (0, 0, 0)),
            pl.BlockSpec((16, width), lambda i: (0, 0)),
        ],
        out_specs=pl.BlockSpec((3, row_count, tile), lambda i: (0, 0, i)),
        scratch_shapes=[
            pltpu.VMEM((row_count, width), BF16),
            pltpu.VMEM((row_count, width), BF16),
            pltpu.VMEM((row_count, 16), F32),
        ],
        name="edge",
    )(rows, cols, edge_weights, none_rows)


def solution(mesh):
    return jax.shard_map(
        on_device,
        mesh=mesh,
        in_specs=(P(None, ("groups", "wide", "narrow"), None), P(), P(), P(), P(), P()),
        out_specs=P("groups", "wide", "narrow"),
        check_vma=False,
    )
```

```python
import functools
import math

import jax
import jax.numpy as jnp
from jax import lax
from jax.experimental import pallas as pl
from jax.experimental.pallas import tpu as pltpu
from jax.sharding import PartitionSpec as P

HEADS = 8
BLOCK = 128
QUERIES = 256
KEYS = 256
F32, BF16 = jnp.float32, jnp.bfloat16
MESH = pl.DeviceIdType.MESH


def layer_norm(values, gain):
    mean = jnp.mean(values, axis=-1, keepdims=True)
    centered = values - mean
    var = jnp.mean(centered * centered, axis=-1, keepdims=True)
    return (centered * lax.rsqrt(var + 1e-05) * gain).astype(BF16)


def project(normed, weight):
    return jnp.dot(normed, weight, preferred_element_type=F32).astype(BF16)


def across(a, b):
    return lax.dot_general(a, b, (((1,), (1,)), ((), ())), preferred_element_type=F32)


def stack_heads(q, stacked):
    head = lax.broadcasted_iota(jnp.int32, q.shape, 1) // (q.shape[1] // HEADS)
    for h in range(HEADS):
        stacked[h * q.shape[0] : (h + 1) * q.shape[0], :] = jnp.where(head == h, q, jnp.zeros_like(q))


def attend_block(stacked, keys_of, values_of, length, same):
    width = stacked.shape[1]
    step = min(KEYS, length)
    count = length // step
    factor = math.log2(math.e) / math.sqrt(width // HEADS)
    q = stacked[...]
    ahead = across(q, keys_of(0, step))
    acc = total = None
    for j in range(count):
        scores = ahead
        if j + 1 < count:
            ahead = across(q, keys_of((j + 1) * step, step))
        expd = jnp.exp2(scores * factor)
        if same is not None:
            expd = jnp.where(same, expd, 0.0)
        part = sum(expd[:, i : i + 128] for i in range(0, step, 128))
        total = part if total is None else total + part
        term = jnp.dot(expd.astype(BF16), values_of(j * step, step), preferred_element_type=F32)
        acc = term if acc is None else acc + term
    inverse = 4.0 / jnp.sum(total, axis=1, keepdims=True)
    acc = acc * inverse * 64.0
    head = lax.broadcasted_iota(jnp.int32, (BLOCK, width), 1) // (width // HEADS)
    out = acc[:BLOCK]
    for h in range(1, HEADS):
        out = jnp.where(head == h, acc[h * BLOCK : (h + 1) * BLOCK], out)
    return out.astype(BF16)


def attend_across(stacked, keys, values):
    length, width = keys.shape
    size = width // HEADS
    step = min(KEYS, length)
    factor = math.log2(math.e) / math.sqrt(size)
    outs = []
    for h in range(HEADS):
        q = stacked[h * QUERIES : (h + 1) * QUERIES, :]
        pieces, total = [], None
        for j in range(0, length, step):
            expd = jnp.exp2(across(keys[j : j + step, :], q) * factor)
            part = jnp.sum(expd.reshape(step // 8, 8, QUERIES), axis=0)
            total = part if total is None else total + part
            pieces.append(expd.astype(BF16))
        acc = jnp.dot(
            values[h * size : (h + 1) * size, :], jnp.concatenate(pieces, axis=0),
            preferred_element_type=F32,
        )
        outs.append(acc * (4.0 / jnp.sum(total, axis=0, keepdims=True)) * 64.0)
    return jnp.transpose(jnp.concatenate(outs, axis=0)).astype(BF16)


def mix_kernel(
    wide, narrow, x_ref, vw_ref, sw_ref, gain_ref, cols_ref, rows_ref,
    q_s, k_s, v_s, x_s, vt_s, queries, stacked, outbox, inbox, pooled, mine,
    send_a, recv_a, send_c, recv_c, send_r, recv_r,
):
    total_vars, width = x_ref.shape
    devices = wide * narrow
    own = total_vars // devices
    per_block = QUERIES // own
    blocks = total_vars // QUERIES
    my_wide, my_narrow = lax.axis_index("wide"), lax.axis_index("narrow")
    me = my_wide * narrow + my_narrow

    def device(d):
        return {"wide": d // narrow, "narrow": lax.rem(d, narrow)}

    barrier = pltpu.get_barrier_semaphore()

    def greet(d, carry):
        @pl.when(d != me)
        def _():
            pl.semaphore_signal(barrier, inc=1, device_id=device(d), device_id_type=MESH)

        return carry

    lax.fori_loop(0, devices, greet, 0)

    def keep(rows, normed, w_ref):
        q_s[rows, :] = project(normed, w_ref[0])
        k_s[rows, :] = project(normed, w_ref[1])
        return project(normed, w_ref[2]).astype(F32) * 2.0**-8

    def prepare(i, carry):
        rows = pl.ds(pl.multiple_of(i * 256, 256), 256)
        v = keep(rows, layer_norm(x_ref[rows, :].astype(F32), gain_ref[0:1, :]), vw_ref)
        vt_s[:, rows] = jnp.transpose(v).astype(BF16)
        return carry

    lax.fori_loop(0, total_vars // 256, prepare, 0)

    my_block = me // per_block

    def post(block):
        def one(j, carry):
            d = block * per_block + j

            @pl.when(d != me)
            def _():
                pltpu.make_async_remote_copy(
                    src_ref=outbox.at[d], dst_ref=inbox.at[me],
                    send_sem=send_a.at[d], recv_sem=recv_a.at[me],
                    device_id=device(d), device_id_type=MESH,
                ).start()

            return carry

        lax.fori_loop(0, per_block, one, 0)

    def variable_block(t):
        block = lax.rem(my_block + 1 + t, blocks)
        rows = pl.ds(pl.multiple_of(block * QUERIES, QUERIES), QUERIES)
        stack_heads(q_s[rows, :], queries)
        out = attend_across(queries, k_s, vt_s)
        update = jnp.dot(out, vw_ref[3], preferred_element_type=F32)
        mixed = x_ref[rows, :].astype(F32) + update
        outbox[pl.ds(block * per_block, per_block)] = mixed.reshape(per_block, own, width).astype(BF16)
        return block

    variable_block(0)
    pl.semaphore_wait(barrier, devices - 1)

    def variable_step(t, carry):
        post(lax.rem(my_block + t, blocks))
        variable_block(t)
        return carry

    lax.fori_loop(1, blocks, variable_step, 0)
    if per_block > 1:
        post(my_block)
    inbox[me] = outbox[me]

    def collect(d, carry):
        @pl.when(d != me)
        def _():
            pltpu.make_async_remote_copy(
                src_ref=outbox.at[d], dst_ref=inbox.at[d],
                send_sem=send_a.at[d], recv_sem=recv_a.at[d],
                device_id=device(d), device_id_type=MESH,
            ).wait()

        return carry

    lax.fori_loop(0, devices, collect, 0)

    tile = 8 * devices
    lump = 16 if own % 16 == 0 else 8

    def prepare_samples(i, carry):
        if lump == own:
            values = inbox[...].astype(F32)
        else:
            values = inbox[:, pl.ds(pl.multiple_of(i * lump, lump), lump), :].astype(F32)
        for half in range(lump // 8):
            start = (i * (lump // 8) + half) * tile
            rows = pl.ds(pl.multiple_of(start, tile), tile)
            tokens = values[:, half * 8 : half * 8 + 8, :].reshape(tile, width)
            x_s[rows, :] = tokens.astype(BF16)
            v = keep(rows, layer_norm(tokens, gain_ref[1:2, :]), sw_ref)
            v_s[rows, :] = v.astype(BF16)
        return carry

    lax.fori_loop(0, own // lump, prepare_samples, 0)
    pooled[...] = jnp.full(pooled.shape, -jnp.inf, F32)
    step = min(KEYS, tile)
    row_var = lax.broadcasted_iota(jnp.int32, (HEADS * BLOCK, step), 0) % 8
    col_var = lax.broadcasted_iota(jnp.int32, (HEADS * BLOCK, step), 1) % 8
    same = row_var == col_var

    def sample_chunk(c, slot):
        rows = pl.ds(pl.multiple_of(c * BLOCK, BLOCK), BLOCK)
        base = c // (tile // BLOCK)
        stack_heads(q_s[rows, :], stacked.at[slot])

        def part(ref):
            return lambda a, n: ref[pl.ds(pl.multiple_of(base * tile + a, BLOCK), n), :]

        out = attend_block(stacked.at[slot], part(k_s), part(v_s), tile, same)
        update = jnp.dot(out, sw_ref[3], preferred_element_type=F32)
        mixed = (x_s[rows, :].astype(F32) + update).astype(BF16).astype(F32)
        best = jnp.max(mixed.reshape(BLOCK // 8, 8, width), axis=0)
        where = pl.ds(pl.multiple_of(base * 8, 8), 8)
        pooled[where, :] = jnp.maximum(pooled[where, :], best)

    piece = min(32, own)
    pieces = own // piece
    per_piece = piece * devices // BLOCK
    unroll = min(stacked.shape[0], per_piece)
    half = devices // narrow
    target = me // half
    slot = lax.rem(me, half)

    def to_cols(w, rows):
        return pltpu.make_async_remote_copy(
            src_ref=mine.at[rows], dst_ref=cols_ref.at[slot, rows],
            send_sem=send_c.at[w], recv_sem=recv_c.at[slot],
            device_id={"wide": w, "narrow": target}, device_id_type=MESH,
        )

    def to_rows(n, rows):
        return pltpu.make_async_remote_copy(
            src_ref=mine.at[rows], dst_ref=rows_ref.at[my_narrow, rows],
            send_sem=send_r.at[n], recv_sem=recv_r.at[my_narrow],
            device_id={"wide": my_wide, "narrow": n}, device_id_type=MESH,
        )

    def each_target(do, rows):
        def one(w, carry):
            @pl.when(w * narrow + target != me)
            def _():
                do(to_cols(w, rows))

            return carry

        lax.fori_loop(0, wide, one, 0)

        def other(n, carry):
            @pl.when(n != my_narrow)
            def _():
                do(to_rows(n, rows))

            return carry

        lax.fori_loop(0, narrow, other, 0)

    def piece_rows(g):
        return pl.ds(pl.multiple_of(g * piece, piece), piece)

    def sample_piece(g, carry):
        if pieces > 1:
            @pl.when(g > 0)
            def _():
                each_target(lambda copy: copy.start(), piece_rows(g - 1))

        def group(i, inner):
            for u in range(unroll):
                sample_chunk(g * per_piece + i * unroll + u, u)
            return inner

        if per_piece == unroll:
            group(0, 0)
        else:
            lax.fori_loop(0, per_piece // unroll, group, 0)
        rows = piece_rows(g)
        mine[rows, :] = layer_norm(pooled[rows, :], gain_ref[2:3, :])
        return carry

    lax.fori_loop(0, pieces, sample_piece, 0)
    each_target(lambda copy: copy.start(), piece_rows(pieces - 1))
    rows_ref[my_narrow] = mine[...]

    @pl.when(target == my_narrow)
    def _():
        cols_ref[slot] = mine[...]

    whole = pl.ds(0, own)
    each_target(lambda copy: copy.wait_send(), whole)

    def arrived(i, carry):
        @pl.when(my_narrow * half + i != me)
        def _():
            pltpu.make_async_remote_copy(
                src_ref=mine, dst_ref=cols_ref.at[i], send_sem=send_c.at[0],
                recv_sem=recv_c.at[i], device_id=device(me), device_id_type=MESH,
            ).wait_recv()

        return carry

    lax.fori_loop(0, half, arrived, 0)

    def beside(n, carry):
        @pl.when(n != my_narrow)
        def _():
            pltpu.make_async_remote_copy(
                src_ref=mine, dst_ref=rows_ref.at[n], send_sem=send_r.at[0],
                recv_sem=recv_r.at[n], device_id=device(me), device_id_type=MESH,
            ).wait_recv()

        return carry

    lax.fori_loop(0, narrow, beside, 0)


def edge_kernel(rows_ref, cols_ref, w_ref, none_ref, out_ref, src_s, dst_s, none_s):
    scale = 1.0 / rows_ref.shape[1] ** 0.5

    @pl.when(pl.program_id(0) == 0)
    def _():
        rows = rows_ref[...]
        src_s[...] = project(rows, w_ref[0])
        dst_s[...] = project(rows, w_ref[1])
        none_s[...] = across(rows, none_ref[...]).astype(BF16).astype(F32)

    cols = cols_ref[...]
    forward = jnp.exp(across(src_s[...], project(cols, w_ref[1])) * scale)
    backward = jnp.exp(across(dst_s[...], project(cols, w_ref[0])) * scale)
    none_cols = across(none_ref[...], cols).astype(BF16).astype(F32)
    absent = jnp.exp(none_s[:, 0:1] + none_cols[0:1, :])
    total = forward + backward + absent
    out_ref[0] = forward / total
    out_ref[1] = backward / total
    out_ref[2] = absent / total


def on_device(states, var_weights, samp_weights, norm_gains, edge_weights, none_weight):
    total_vars, samp_local, width = states.shape
    wide, narrow = lax.axis_size("wide"), lax.axis_size("narrow")
    devices = wide * narrow
    own = total_vars // devices
    assert samp_local == 1 and BLOCK % own == 0 and own % 8 == 0
    half = devices // narrow
    vmem = pl.BlockSpec(memory_space=pltpu.VMEM)
    dma = pltpu.SemaphoreType.DMA
    cols, rows = pl.pallas_call(
        functools.partial(mix_kernel, wide, narrow),
        out_shape=(
            jax.ShapeDtypeStruct((half, own, width), BF16),
            jax.ShapeDtypeStruct((narrow, own, width), BF16),
        ),
        in_specs=[vmem] * 4,
        out_specs=(vmem, vmem),
        scratch_shapes=[pltpu.VMEM((total_vars, width), BF16)] * 4
        + [
            pltpu.VMEM((width, total_vars), BF16),
            pltpu.VMEM((HEADS * QUERIES, width), BF16),
            pltpu.VMEM((4, HEADS * BLOCK, width), BF16),
            pltpu.VMEM((devices, own, width), BF16),
            pltpu.VMEM((devices, own, width), BF16),
            pltpu.VMEM((own, width), F32),
            pltpu.VMEM((own, width), BF16),
            dma((devices,)), dma((devices,)), dma((wide,)), dma((half,)),
            dma((narrow,)), dma((narrow,)),
        ],
        compiler_params=pltpu.CompilerParams(
            collective_id=0, has_side_effects=True, vmem_limit_bytes=60 * 2**20
        ),
        name="mix",
    )(states.reshape(total_vars, width), var_weights, samp_weights, norm_gains)
    cols = cols.reshape(half * own, width)
    rows = rows.reshape(narrow * own, width)
    row_count, col_count = narrow * own, half * own
    tile = min(256, col_count)
    none_rows = jnp.broadcast_to(none_weight[None, :], (16, width))
    return pl.pallas_call(
        edge_kernel,
        grid=(col_count // tile,),
        out_shape=jax.ShapeDtypeStruct((3, row_count, col_count), F32),
        in_specs=[
            pl.BlockSpec((row_count, width), lambda i: (0, 0)),
            pl.BlockSpec((tile, width), lambda i: (i, 0)),
            pl.BlockSpec((2, width, width), lambda i: (0, 0, 0)),
            pl.BlockSpec((16, width), lambda i: (0, 0)),
        ],
        out_specs=pl.BlockSpec((3, row_count, tile), lambda i: (0, 0, i)),
        scratch_shapes=[
            pltpu.VMEM((row_count, width), BF16),
            pltpu.VMEM((row_count, width), BF16),
            pltpu.VMEM((row_count, 16), F32),
        ],
        name="edge",
    )(rows, cols, edge_weights, none_rows)


def solution(mesh):
    return jax.shard_map(
        on_device,
        mesh=mesh,
        in_specs=(P(None, ("groups", "wide", "narrow"), None), P(), P(), P(), P(), P()),
        out_specs=P("groups", "wide", "narrow"),
        check_vma=False,
    )
```
